32 devices in a mesh: ctx: 8 (over z, x), fsdp: 4 (over y, core).
Axes of the slice: x: 2, y: 2, z: 4, core: 2. Of those that a mesh axis runs over, the one named last changes fastest.
Arguments:
- layer_in: float32 [4, 1024, 1536], P('fsdp', 'ctx'), may hold values from -6 to 6
- block_map: int32 [16], replicated, may hold values from 0 to 15, each once
- attn_gain: bfloat16 [1536], P('fsdp'), may hold values from 0.5 to 1.5
- query_weight: bfloat16 [1536, 1536], P('fsdp'), may hold values from -0.15625 to 0.15625
- query_bias: bfloat16 [1536], P('fsdp'), may hold values from -3 to 3
- key_weight: bfloat16 [1536, 256], P('fsdp'), may hold values from -0.15625 to 0.15625
- key_bias: bfloat16 [256], P('fsdp'), may hold values from -3 to 3
- value_weight: bfloat16 [1536, 256], P('fsdp'), may hold values from -0.15625 to 0.15625
- value_bias: bfloat16 [256], P('fsdp'), may hold values from -3 to 3
- out_weight: bfloat16 [1536, 1536], P('fsdp'), may hold values from -1.25 to 1.25
- mlp_gain: bfloat16 [1536], P('fsdp'), may hold values from 0.5 to 1.5
- gate_weight: bfloat16 [1536, 8960], P('fsdp'), may hold values from -0.15625 to 0.15625
- up_weight: bfloat16 [1536, 8960], P('fsdp'), may hold values from -0.15625 to 0.15625
- down_weight: bfloat16 [1536, 8960], P('fsdp'), may hold values from -0.0625 to 0.0625
- out_grad: float32 [4, 1024, 1536], P('fsdp', 'ctx'), may hold values from -6 to 6
Outputs:
- layer_out: float32 [4, 1024, 1536], P('fsdp', 'ctx')
- in_grad: float32 [4, 1024, 1536], P('fsdp', 'ctx')
- attn_gain_grad: float32 [1536], P(('ctx', 'fsdp'))
- query_weight_grad: float32 [1536, 1536], P(('ctx', 'fsdp'))
- query_bias_grad: float32 [1536], P(('ctx', 'fsdp'))
- key_weight_grad: float32 [1536, 256], P(('ctx', 'fsdp'))
- key_bias_grad: float32 [256], P(('ctx', 'fsdp'))
- value_weight_grad: float32 [1536, 256], P(('ctx', 'fsdp'))
- value_bias_grad: float32 [256], P(('ctx', 'fsdp'))
- out_weight_grad: float32 [1536, 1536], P(('ctx', 'fsdp'))
- mlp_gain_grad: float32 [1536], P(('ctx', 'fsdp'))
- gate_weight_grad: float32 [1536, 8960], P(('ctx', 'fsdp'))
- up_weight_grad: float32 [1536, 8960], P(('ctx', 'fsdp'))
- down_weight_grad: float32 [1536, 8960], P(('ctx', 'fsdp'))
The draws below stay inside these ranges and needn't reach their ends.
Inputs may be any that keep to these rules, and one draw needn't show every extreme that they name: block_map is a permutation; the device at index c of ctx holds position blocks block_map[2 c] and block_map[2 c + 1] of its sequence, each of 64 tokens.
All inputs are finite; a program needn't handle non-finite values.
Results may differ from the reference program's by a relative error of at most 0.019.
Values may be sent and summed in bfloat16 or wider, within the bound.
No kernel may reach another device: no remote copies, remote signals or barrier semaphores. Data moves between devices by JAX's collectives and lax.ppermute only.
A program may use at most 320 MiB of HBM per device.

```python
import math
import jax
import jax.numpy as jnp
from jax import lax

D = 1536
FF = 8960
HEADS = 12
KV_HEADS = 2
HEAD_DIM = 128
TOK_DEV = 128
LENGTH = 1024
SEQS = 4
N_CTX = 8


def levels(key, dims, shards, smallest, top_value):
    def one(dim, blocks):
        steps = jax.random.uniform(jax.random.fold_in(jax.random.fold_in(key, 6), dim), (blocks,), jnp.float32, smallest / len(shards), top_value / len(shards))
        return jnp.repeat(jnp.exp(steps), dims[dim] // blocks).reshape((-1,) + (1,) * (len(dims) - dim - 1))

    factor_of = one(*shards[0])
    for cut in shards[1:]:
        factor_of = factor_of * one(*cut)
    return factor_of


def bell_draw(key, dims, spread, bound, split=(), kind=jnp.bfloat16):
    level = levels(key, dims, split, -0.22, 0.18) if split else 1.0
    array = jax.random.normal(key, dims, jnp.float32) * spread * level
    return jnp.minimum(jnp.maximum(array, -bound), bound).astype(kind)


def setup_inputs(seed: int = 0) -> dict:
    keys = jax.random.split(jax.random.key(seed), 16)
    layer_in = bell_draw(keys[0], (SEQS, LENGTH, D), 1.0, 6.0, ((0, 4), (1, 8)), jnp.float32)
    block_map = jax.random.permutation(keys[1], 2 * N_CTX).astype(jnp.int32)
    attn_gain = jnp.clip(1.0 + 0.1 * jax.random.normal(keys[2], (D,), jnp.float32), 0.5, 1.5).astype(jnp.bfloat16)
    query_weight = bell_draw(keys[3], (D, HEADS * HEAD_DIM), D ** -0.5, 0.15625, ((0, 4),))
    query_bias = bell_draw(keys[4], (HEADS * HEAD_DIM,), 0.5, 3.0, ((0, 4),))
    key_weight = bell_draw(keys[5], (D, KV_HEADS * HEAD_DIM), D ** -0.5, 0.15625, ((0, 4),))
    key_bias = bell_draw(keys[6], (KV_HEADS * HEAD_DIM,), 0.5, 3.0, ((0, 4),))
    value_weight = bell_draw(keys[7], (D, KV_HEADS * HEAD_DIM), D ** -0.5, 0.15625, ((0, 4),))
    value_bias = bell_draw(keys[8], (KV_HEADS * HEAD_DIM,), 0.5, 3.0, ((0, 4),))
    out_weight = bell_draw(keys[9], (D, HEADS * HEAD_DIM), (max(1, HEADS * HEAD_DIM * 16 // (TOK_DEV * N_CTX))) ** -0.5, 1.25, ((0, 4),))
    mlp_gain = jnp.clip(1.0 + 0.1 * jax.random.normal(keys[10], (D,), jnp.float32), 0.5, 1.5).astype(jnp.bfloat16)
    gate_weight = bell_draw(keys[11], (D, FF), D ** -0.5, 0.15625, ((0, 4),))
    up_weight = bell_draw(keys[12], (D, FF), D ** -0.5, 0.15625, ((0, 4),))
    down_weight = bell_draw(keys[13], (D, FF), FF ** -0.5, 0.0625, ((0, 4),))
    out_grad = bell_draw(keys[14], (SEQS, LENGTH, D), 1.0, 6.0, ((0, 4), (1, 8)), jnp.float32)
    return dict(layer_in=layer_in, block_map=block_map, attn_gain=attn_gain, query_weight=query_weight, query_bias=query_bias, key_weight=key_weight, key_bias=key_bias, value_weight=value_weight, value_bias=value_bias, out_weight=out_weight, mlp_gain=mlp_gain, gate_weight=gate_weight, up_weight=up_weight, down_weight=down_weight, out_grad=out_grad)


NORM_EPSILON = 1e-06
ROPE_THETA = 1000000.0
MASK_VALUE = -1e+30

def rounded(values):
    return lax.optimization_barrier(values.astype(jnp.bfloat16))

def dot_rows(left_side, right_side):
    return lax.dot_general(left_side, right_side, (((1,), (1,)), ((), ())), preferred_element_type=jnp.float32)

def dot_cols(left_side, right_side):
    return lax.dot_general(left_side, right_side, (((0,), (0,)), ((), ())), preferred_element_type=jnp.float32)

def by_ctx(values, seq_count):
    width_now = values.shape[-1]
    grouped = values.reshape(seq_count, N_CTX, -1, width_now)
    return jnp.transpose(grouped, (1, 0, 2, 3)).reshape(N_CTX, -1, width_now)

def from_ctx(values, seq_count):
    width_now = values.shape[-1]
    grouped = values.reshape(N_CTX, seq_count, -1, width_now)
    return jnp.transpose(grouped, (1, 0, 2, 3)).reshape(-1, width_now)

def ctx_sum(left_side, right_side, seq_count):

    def add_one(total, pair):
        return (total + rounded(dot_cols(pair[0], pair[1])).astype(jnp.float32), None)
    start = jnp.zeros((left_side.shape[1], right_side.shape[1]), jnp.float32)
    total, _ = lax.scan(add_one, start, (by_ctx(left_side, seq_count), by_ctx(right_side, seq_count)))
    return total

def rms_scale(values):
    return lax.rsqrt(lax.optimization_barrier(jnp.mean(values * values, axis=-1, keepdims=True)) + NORM_EPSILON)

def norm_back(upstream, values, inv_rms, gain_vec):
    weighted = upstream * gain_vec.astype(jnp.float32)
    gain_part = lax.optimization_barrier(jnp.sum(upstream * values * inv_rms, axis=0))
    inner_mean = lax.optimization_barrier(jnp.mean(weighted * values, axis=-1, keepdims=True))
    return (inv_rms * weighted - values * (inv_rms * inv_rms * inv_rms) * inner_mean, gain_part)

def rope_tables(token_pos, head_dim):
    half_dim = head_dim // 2
    inv_freq = ROPE_THETA ** (jnp.arange(half_dim, dtype=jnp.float32) * (-2.0 / head_dim))
    angles = token_pos.astype(jnp.float32)[:, None] * inv_freq[None, :]
    angles = jnp.concatenate([angles, angles], axis=1)
    return (jnp.cos(angles), jnp.sin(angles))

def rotate(heads_in, cos_tab, sin_tab):
    half_dim = heads_in.shape[-1] // 2
    turned = jnp.concatenate([-heads_in[..., half_dim:], heads_in[..., :half_dim]], axis=-1)
    return heads_in * cos_tab[:, None, :] + turned * sin_tab[:, None, :]

def unrotate(grad_vals, cos_tab, sin_tab):
    half_dim = grad_vals.shape[-1] // 2
    scaled = grad_vals * sin_tab[:, None, :]
    back_turn = jnp.concatenate([scaled[..., half_dim:], -scaled[..., :half_dim]], axis=-1)
    return grad_vals * cos_tab[:, None, :] + back_turn

def masked_scores(query_part, pos_part, keys_wide, token_pos):
    scores = jnp.einsum('qgha,kga->ghqk', query_part.astype(jnp.float32), keys_wide) * HEAD_DIM ** (-0.5)
    allowed = token_pos[None, :] <= pos_part[:, None]
    return jnp.where(allowed, scores, MASK_VALUE)

def attend_forward(query_seq, keys_seq, values_seq, token_pos):
    length_now = query_seq.shape[0]
    row_block = math.gcd(length_now, 512)
    keys_wide = keys_seq.astype(jnp.float32)
    values_wide = values_seq.astype(jnp.float32)

    def one_block(block_in):
        query_part, pos_part = block_in
        scores = masked_scores(query_part, pos_part, keys_wide, token_pos)
        row_max = lax.optimization_barrier(jnp.max(scores, axis=-1, keepdims=True))
        log_norm = row_max + jnp.log(lax.optimization_barrier(jnp.sum(jnp.exp(scores - row_max), axis=-1, keepdims=True)))
        probs_low = rounded(jnp.exp(scores - log_norm))
        attended = jnp.einsum('ghqk,kga->qgha', probs_low.astype(jnp.float32), values_wide)
        return (rounded(attended), log_norm[..., 0])
    blocks_in = (query_seq.reshape((length_now // row_block, row_block) + query_seq.shape[1:]), token_pos.reshape(length_now // row_block, row_block))
    return lax.map(one_block, blocks_in)

def attend_backward(query_seq, keys_seq, values_seq, token_pos, attended, log_norm, grad_seq):
    length_now = query_seq.shape[0]
    row_block = math.gcd(length_now, 512)
    score_scale = HEAD_DIM ** (-0.5)
    keys_wide = keys_seq.astype(jnp.float32)
    values_wide = values_seq.astype(jnp.float32)

    def one_block(carried, block_in):
        key_acc, value_acc = carried
        query_part, pos_part, out_part, norm_part, grad_part = block_in
        scores = masked_scores(query_part, pos_part, keys_wide, token_pos)
        prob_vals = jnp.exp(scores - norm_part[..., None])
        grad_wide = grad_part.astype(jnp.float32)
        row_delta = jnp.transpose(lax.optimization_barrier(jnp.sum(grad_wide * out_part.astype(jnp.float32), axis=-1)), (1, 2, 0))
        grad_probs = jnp.einsum('qgha,kga->ghqk', grad_wide, values_wide)
        grad_scores = rounded(prob_vals * (grad_probs - row_delta[..., None])).astype(jnp.float32)
        probs_low = rounded(prob_vals).astype(jnp.float32)
        grad_query = score_scale * jnp.einsum('ghqk,kga->qgha', grad_scores, keys_wide)
        key_acc = key_acc + score_scale * jnp.einsum('ghqk,qgha->kga', grad_scores, query_part.astype(jnp.float32))
        value_acc = value_acc + jnp.einsum('ghqk,qgha->kga', probs_low, grad_wide)
        return ((key_acc, value_acc), grad_query)
    count_now = length_now // row_block
    blocks_in = (query_seq.reshape((count_now, row_block) + query_seq.shape[1:]), token_pos.reshape(count_now, row_block), attended, log_norm, grad_seq.reshape((count_now, row_block) + grad_seq.shape[1:]))
    zeros_keys = jnp.zeros(keys_seq.shape, jnp.float32)
    (grad_keys, grad_values), grad_query = lax.scan(one_block, (zeros_keys, zeros_keys), blocks_in)
    return (grad_query, grad_keys, grad_values)

def reference(layer_in, block_map, attn_gain, query_weight, query_bias, key_weight, key_bias, value_weight, value_bias, out_weight, mlp_gain, gate_weight, up_weight, down_weight, out_grad):
    seq_count, seq_length, model_width = layer_in.shape
    total_rows = seq_count * seq_length
    group_size = HEADS // KV_HEADS
    query_width = HEADS * HEAD_DIM
    key_width = KV_HEADS * HEAD_DIM
    inputs = layer_in.reshape(total_rows, model_width)
    cotangent = out_grad.reshape(total_rows, model_width)
    block_len = seq_length // block_map.shape[0]
    stored = jnp.arange(seq_length, dtype=jnp.int32)
    token_pos = (block_map[stored // block_len] * block_len + stored % block_len).astype(jnp.int32)
    cos_seq, sin_seq = rope_tables(token_pos, HEAD_DIM)
    cos_tab = jnp.tile(cos_seq, (seq_count, 1))
    sin_tab = jnp.tile(sin_seq, (seq_count, 1))
    inv_one = rms_scale(inputs)
    normed_one = rounded(inputs * inv_one * attn_gain.astype(jnp.float32))
    query_lin = jnp.dot(normed_one, query_weight, preferred_element_type=jnp.float32) + query_bias.astype(jnp.float32)
    key_lin = jnp.dot(normed_one, key_weight, preferred_element_type=jnp.float32) + key_bias.astype(jnp.float32)
    value_low = rounded(jnp.dot(normed_one, value_weight, preferred_element_type=jnp.float32) + value_bias.astype(jnp.float32))
    query_low = rounded(rotate(query_lin.reshape(total_rows, HEADS, HEAD_DIM), cos_tab, sin_tab))
    key_low = rounded(rotate(key_lin.reshape(total_rows, KV_HEADS, HEAD_DIM), cos_tab, sin_tab))
    query_seqs = query_low.reshape(seq_count, seq_length, KV_HEADS, group_size, HEAD_DIM)
    key_seqs = key_low.reshape(seq_count, seq_length, KV_HEADS, HEAD_DIM)
    value_seqs = value_low.reshape(seq_count, seq_length, KV_HEADS, HEAD_DIM)

    def forward_seq(seq_in):
        return attend_forward(seq_in[0], seq_in[1], seq_in[2], token_pos)
    attended, log_norm = lax.map(forward_seq, (query_seqs, key_seqs, value_seqs))
    attn_out = attended.reshape(total_rows, query_width)
    resid_one = inputs + dot_rows(attn_out, out_weight)
    ff_width = gate_weight.shape[1]

    def mlp_block(carried, block_in):
        gate_acc, up_acc, down_acc, gain_acc = carried
        resid_part, grad_part = block_in
        inv_two = rms_scale(resid_part)
        normed_two = rounded(resid_part * inv_two * mlp_gain.astype(jnp.float32))
        gate_lin = jnp.dot(normed_two, gate_weight, preferred_element_type=jnp.float32)
        up_lin = jnp.dot(normed_two, up_weight, preferred_element_type=jnp.float32)
        sig_gate = jax.nn.sigmoid(gate_lin)
        activated = gate_lin * sig_gate
        hidden = rounded(activated * up_lin)
        result = resid_part + dot_rows(hidden, down_weight)
        grad_low = rounded(grad_part)
        grad_hidden = jnp.dot(grad_low, down_weight, preferred_element_type=jnp.float32)
        grad_gate = rounded(grad_hidden * up_lin * (sig_gate * (1.0 + gate_lin * (1.0 - sig_gate))))
        grad_up = rounded(grad_hidden * activated)
        grad_normed = dot_rows(grad_gate, gate_weight) + dot_rows(grad_up, up_weight)
        grad_resid, gain_part = norm_back(grad_normed, resid_part, inv_two, mlp_gain)
        carried = (gate_acc + rounded(dot_cols(normed_two, grad_gate)).astype(jnp.float32), up_acc + rounded(dot_cols(normed_two, grad_up)).astype(jnp.float32), down_acc + rounded(dot_cols(grad_low, hidden)).astype(jnp.float32), gain_acc + gain_part)
        return (carried, (result, grad_part + grad_resid))
    zeros_ff = jnp.zeros((model_width, ff_width), jnp.float32)
    carry_init = (zeros_ff, zeros_ff, zeros_ff, jnp.zeros((model_width,), jnp.float32))
    (gate_grad, up_grad, down_grad, mlp_gain_grad), (layer_rows, resid_grad) = lax.scan(mlp_block, carry_init, (by_ctx(resid_one, seq_count), by_ctx(cotangent, seq_count)))
    layer_rows = from_ctx(layer_rows, seq_count)
    resid_grad = from_ctx(resid_grad, seq_count)
    resid_low = rounded(resid_grad)
    out_weight_grad = ctx_sum(resid_low, attn_out, seq_count)
    grad_attn = rounded(jnp.dot(resid_low, out_weight, preferred_element_type=jnp.float32))
    grad_seqs = grad_attn.reshape(seq_count, seq_length, KV_HEADS, group_size, HEAD_DIM)

    def backward_seq(seq_in):
        return attend_backward(seq_in[0], seq_in[1], seq_in[2], token_pos, seq_in[3], seq_in[4], seq_in[5])
    grad_query, grad_keys, grad_values = lax.map(backward_seq, (query_seqs, key_seqs, value_seqs, attended, log_norm, grad_seqs))
    query_pre = unrotate(grad_query.reshape(total_rows, HEADS, HEAD_DIM), cos_tab, sin_tab).reshape(total_rows, query_width)
    key_pre = unrotate(grad_keys.reshape(total_rows, KV_HEADS, HEAD_DIM), cos_tab, sin_tab).reshape(total_rows, key_width)
    value_pre = grad_values.reshape(total_rows, key_width)
    query_grad_low = rounded(query_pre)
    key_grad_low = rounded(key_pre)
    value_grad_low = rounded(value_pre)
    grad_normed_one = dot_rows(query_grad_low, query_weight) + dot_rows(key_grad_low, key_weight) + dot_rows(value_grad_low, value_weight)
    grad_inputs, attn_gain_grad = norm_back(grad_normed_one, inputs, inv_one, attn_gain)
    in_grad = resid_grad + grad_inputs
    return (layer_rows.reshape(layer_in.shape), in_grad.reshape(layer_in.shape), attn_gain_grad, ctx_sum(normed_one, query_grad_low, seq_count), lax.optimization_barrier(jnp.sum(query_pre, axis=0)), ctx_sum(normed_one, key_grad_low, seq_count), lax.optimization_barrier(jnp.sum(key_pre, axis=0)), ctx_sum(normed_one, value_grad_low, seq_count), lax.optimization_barrier(jnp.sum(value_pre, axis=0)), out_weight_grad, mlp_gain_grad, gate_grad, up_grad, down_grad)
```

```python
import jax
import jax.numpy as jnp
from jax import lax
from jax.sharding import PartitionSpec as P

HEADS = 12
KV_HEADS = 2
HEAD_DIM = 128
GROUP = HEADS // KV_HEADS

NORM_EPSILON = 1e-06
ROPE_THETA = 1000000.0
MASK_VALUE = -1e30
LANES = 128

bf16 = jnp.bfloat16
f32 = jnp.float32


def dot_plain(left_side, right_side):
    return jnp.dot(left_side, right_side, preferred_element_type=f32)


def dot_rows(left_side, right_side):
    return lax.dot_general(
        left_side, right_side, (((1,), (1,)), ((), ())), preferred_element_type=f32
    )


def dot_cols(left_side, right_side):
    return lax.dot_general(
        left_side, right_side, (((0,), (0,)), ((), ())), preferred_element_type=f32
    )


def rms_scale(values):
    return lax.rsqrt(jnp.mean(values * values, axis=-1, keepdims=True) + NORM_EPSILON)


def norm_back(upstream, values, inv_rms, gain_vec):
    weighted = upstream * gain_vec
    gain_part = jnp.sum(upstream * values * inv_rms, axis=0)
    inner_mean = jnp.mean(weighted * values, axis=-1, keepdims=True)
    return (inv_rms * weighted - values * (inv_rms * inv_rms * inv_rms) * inner_mean, gain_part)


def rope_tables(token_pos, head_dim):
    half_dim = head_dim // 2
    inv_freq = ROPE_THETA ** (jnp.arange(half_dim, dtype=f32) * (-2.0 / head_dim))
    angles = token_pos.astype(f32)[:, None] * inv_freq[None, :]
    angles = jnp.concatenate([angles, angles], axis=1)
    return (jnp.cos(angles), jnp.sin(angles))


def rotate(heads_in, cos_tab, sin_tab):
    half_dim = heads_in.shape[-1] // 2
    turned = jnp.concatenate([-heads_in[..., half_dim:], heads_in[..., :half_dim]], axis=-1)
    return heads_in * cos_tab[:, None, :] + turned * sin_tab[:, None, :]


def unrotate(grad_vals, cos_tab, sin_tab):
    half_dim = grad_vals.shape[-1] // 2
    scaled = grad_vals * sin_tab[:, None, :]
    back_turn = jnp.concatenate([scaled[..., half_dim:], -scaled[..., :half_dim]], axis=-1)
    return grad_vals * cos_tab[:, None, :] + back_turn


class Links:
    def __init__(self):
        self.count = lax.axis_size("ctx")
        self.rank = lax.axis_index("ctx")
        self.seq = lax.axis_index("fsdp")
        count = self.count
        if count == 8:
            self.ring = [0, 2, 4, 6, 7, 5, 3, 1]
        else:
            self.ring = list(range(count))
        following = {self.ring[i]: self.ring[(i + 1) % count] for i in range(count)}
        self.ahead = [(i, following[i]) for i in range(count)]
        self.back = [(following[i], i) for i in range(count)]
        place = [self.ring.index(i) for i in range(count)]
        half = count // 2
        self.offsets = [0] + [s * k for k in range(1, half) for s in (1, -1)] + [half]
        ring_arr = jnp.array(self.ring, jnp.int32)
        my_place = jnp.array(place, jnp.int32)[self.rank]
        self.order = [ring_arr[(my_place + off) % count] for off in self.offsets]

    def forward(self, values):
        return lax.ppermute(values, "ctx", self.ahead)

    def backward(self, values):
        return lax.ppermute(values, "ctx", self.back)

    def core(self, values):
        return lax.ppermute(values, "fsdp", [(i, i ^ 1) for i in range(4)])

    def chip(self, values):
        return lax.ppermute(values, "fsdp", [(i, i ^ 2) for i in range(4)])

    def gather_fsdp(self, values):
        near = self.core(values)
        far = self.chip(values)
        return [values, near, far, self.core(far)]

    def gather_ring(self, values):
        half_rows = values.shape[0] // 2
        half = self.count // 2
        found = {0: values}
        going, coming = values, values
        for k in range(1, half):
            going, coming = self.forward(going), self.backward(coming)
            found[-k], found[k] = going, coming
        far_low = self.forward(going[:half_rows])
        far_high = self.backward(coming[half_rows:])
        found[half] = jnp.concatenate([far_low, far_high], axis=0)
        return [found[off] for off in self.offsets]

    def reduce_ring(self, blocks):
        part = dict(zip(self.offsets, blocks))
        half = self.count // 2
        half_rows = blocks[0].shape[0] // 2
        going = self.forward(part[half][:half_rows])
        coming = self.backward(part[half][half_rows:])
        top, bottom = part[half - 1], part[1 - half]
        going = jnp.concatenate([top[:half_rows] + going, top[half_rows:]], axis=0)
        coming = jnp.concatenate([bottom[:half_rows], bottom[half_rows:] + coming], axis=0)
        for k in range(half - 2, -1, -1):
            going, coming = self.forward(going), self.backward(coming)
            if k:
                going, coming = going + part[k], coming + part[-k]
        return part[0].astype(f32) + going.astype(f32) + coming.astype(f32)


def shards(
    layer_in,
    block_map,
    attn_gain,
    query_weight,
    query_bias,
    key_weight,
    key_bias,
    value_weight,
    value_bias,
    out_weight,
    mlp_gain,
    gate_weight,
    up_weight,
    down_weight,
    out_grad,
):
    links = Links()
    ctx_count, fsdp_count = links.count, 4
    ctx_rank, fsdp_rank = links.rank, links.seq
    tok_rows, model_width = layer_in.shape[1:]
    ff_width = gate_weight.shape[1]
    block_len = tok_rows // 2
    seq_length = tok_rows * ctx_count
    query_width = HEADS * HEAD_DIM
    key_width = KV_HEADS * HEAD_DIM
    quarter = model_width // fsdp_count
    rows_each = model_width // (ctx_count * fsdp_count)
    groups_each = ctx_count // fsdp_count
    score_scale = HEAD_DIM ** (-0.5)

    def turn_cols(values):
        return jnp.concatenate(
            [
                lax.dynamic_slice_in_dim(values, (fsdp_rank ^ j) * quarter, quarter, values.ndim - 1)
                for j in range(fsdp_count)
            ],
            axis=-1,
        )

    tiles = ff_width // LANES
    span = -(-tiles // ctx_count)
    first_tile = jnp.minimum(span * ctx_rank, tiles - span)
    skipped = span * ctx_rank - first_tile
    width = span * LANES

    def ff_slice(weight):
        return lax.dynamic_slice_in_dim(weight, first_tile * LANES, width, 1)

    inputs = turn_cols(layer_in[0])
    cotangent = turn_cols(out_grad[0])
    grad_low = cotangent.astype(bf16)

    small_in = jnp.concatenate([attn_gain, mlp_gain, query_bias, key_bias, value_bias])
    small_rows = jnp.zeros((8 * 2 * key_width,), bf16).at[: small_in.shape[0]].set(small_in)
    first_msg = jnp.concatenate(
        [
            jnp.concatenate([key_weight, value_weight], axis=1),
            small_rows.reshape(8, 2 * key_width),
        ],
        axis=0,
    )
    first_all = links.gather_fsdp(first_msg)
    query_all = links.gather_fsdp(query_weight)
    out_all = links.gather_fsdp(out_weight)
    down_all = links.gather_fsdp(ff_slice(down_weight))
    gate_all = links.gather_fsdp(ff_slice(gate_weight))
    up_all = links.gather_fsdp(ff_slice(up_weight))

    key_value_w = jnp.concatenate([piece[:quarter] for piece in first_all], axis=0)
    small_all = [piece[quarter:].reshape(-1) for piece in first_all]
    q_each, k_each = query_width // fsdp_count, key_width // fsdp_count
    attn_gain_all = jnp.concatenate([s[:quarter] for s in small_all]).astype(f32)
    mlp_gain_all = jnp.concatenate([s[quarter : 2 * quarter] for s in small_all]).astype(f32)
    stacked = jnp.stack(small_all)
    ordered = jnp.concatenate(
        [lax.dynamic_index_in_dim(stacked, fsdp_rank ^ j, 0) for j in range(fsdp_count)], axis=0
    )
    bias_at = 2 * quarter
    query_b = ordered[:, bias_at : bias_at + q_each].reshape(-1).astype(f32)
    key_b = ordered[:, bias_at + q_each : bias_at + q_each + k_each].reshape(-1).astype(f32)
    value_b = (
        ordered[:, bias_at + q_each + k_each : bias_at + q_each + 2 * k_each]
        .reshape(-1)
        .astype(f32)
    )
    query_w = jnp.concatenate(query_all, axis=0)
    out_w = jnp.concatenate(out_all, axis=0)
    down_w = jnp.concatenate(down_all, axis=0)
    gate_w = jnp.concatenate(gate_all, axis=0)
    up_w = jnp.concatenate(up_all, axis=0)

    block_pairs = block_map.reshape(ctx_count, 2)
    offsets = jnp.arange(block_len, dtype=jnp.int32)
    key_blocks = jnp.stack(
        [lax.dynamic_index_in_dim(block_pairs, at, 0, keepdims=False) for at in links.order]
    )
    key_pos = (key_blocks.reshape(-1, 1) * block_len + offsets[None, :]).reshape(seq_length)
    token_pos = key_pos[:tok_rows]
    cos_tab, sin_tab = rope_tables(token_pos, HEAD_DIM)

    inv_one = rms_scale(inputs)
    normed_one = (inputs * inv_one * attn_gain_all).astype(bf16)
    key_value_lin = dot_plain(normed_one, key_value_w)
    key_lin = key_value_lin[:, :key_width] + key_b
    value_low = (key_value_lin[:, key_width:] + value_b).astype(bf16)
    key_low = (
        rotate(key_lin.reshape(tok_rows, KV_HEADS, HEAD_DIM), cos_tab, sin_tab)
        .astype(bf16)
        .reshape(tok_rows, key_width)
    )
    key_value_all = jnp.concatenate(
        links.gather_ring(jnp.concatenate([key_low, value_low], axis=1)), axis=0
    )
    grad_low_blocks = links.gather_ring(grad_low)
    keys_all = key_value_all[:, :key_width].reshape(seq_length, KV_HEADS, HEAD_DIM)
    values_all = key_value_all[:, key_width:].reshape(seq_length, KV_HEADS, HEAD_DIM)

    query_lin = dot_plain(normed_one, query_w) + query_b
    query_low = rotate(query_lin.reshape(tok_rows, HEADS, HEAD_DIM), cos_tab, sin_tab).astype(bf16)
    query_group = query_low.reshape(tok_rows, KV_HEADS, GROUP, HEAD_DIM)
    scores = (
        jnp.einsum("qgha,kga->ghqk", query_group, keys_all, preferred_element_type=f32)
        * score_scale
    )
    allowed = key_pos[None, :] <= token_pos[:, None]
    scores = jnp.where(allowed, scores, MASK_VALUE)
    row_max = jnp.max(scores, axis=-1, keepdims=True)
    log_norm = row_max + jnp.log(jnp.sum(jnp.exp(scores - row_max), axis=-1, keepdims=True))
    prob_vals = jnp.exp(scores - log_norm)
    probs_low = prob_vals.astype(bf16)
    attn_out = (
        jnp.einsum("ghqk,kga->qgha", probs_low, values_all, preferred_element_type=f32)
        .reshape(tok_rows, query_width)
        .astype(bf16)
    )
    resid_one = inputs + dot_rows(attn_out, out_w)
    inv_two = rms_scale(resid_one)
    normed_two = (resid_one * inv_two * mlp_gain_all).astype(bf16)

    normed_two_all = jnp.concatenate(links.gather_ring(normed_two), axis=0)
    grad_low_all = jnp.concatenate(grad_low_blocks, axis=0)
    kept = (lax.broadcasted_iota(jnp.int32, (1, width), 1) // LANES) >= skipped
    grad_hidden = dot_plain(grad_low_all, down_w)
    gate_lin = dot_plain(normed_two_all, gate_w)
    up_lin = dot_plain(normed_two_all, up_w)
    sig_gate = jax.nn.sigmoid(gate_lin)
    activated = gate_lin * sig_gate
    hidden = jnp.where(kept, activated * up_lin, 0.0).astype(bf16)
    grad_gate = jnp.where(
        kept, grad_hidden * up_lin * (sig_gate * (1.0 + gate_lin * (1.0 - sig_gate))), 0.0
    ).astype(bf16)
    grad_up = jnp.where(kept, grad_hidden * activated, 0.0).astype(bf16)
    grad_normed_part = (dot_rows(grad_gate, gate_w) + dot_rows(grad_up, up_w)).astype(bf16)
    mlp_part = dot_rows(hidden, down_w).astype(bf16)

    def blocks_of(values):
        return [values[i * tok_rows : (i + 1) * tok_rows] for i in range(ctx_count)]

    grad_normed_two = links.reduce_ring(blocks_of(grad_normed_part))
    grad_resid, mlp_gain_part = norm_back(grad_normed_two, resid_one, inv_two, mlp_gain_all)
    resid_grad = cotangent + grad_resid
    resid_low = resid_grad.astype(bf16)

    grad_attn = dot_plain(resid_low, out_w).astype(bf16)
    grad_group = grad_attn.reshape(tok_rows, KV_HEADS, GROUP, HEAD_DIM)
    attn_group = attn_out.reshape(tok_rows, KV_HEADS, GROUP, HEAD_DIM)
    row_delta = jnp.transpose(
        jnp.sum(grad_group.astype(f32) * attn_group.astype(f32), axis=-1), (1, 2, 0)
    )
    grad_probs = jnp.einsum("qgha,kga->ghqk", grad_group, values_all, preferred_element_type=f32)
    grad_scores = (prob_vals * (grad_probs - row_delta[..., None])).astype(bf16)
    grad_query = score_scale * jnp.einsum(
        "ghqk,kga->qgha", grad_scores, keys_all, preferred_element_type=f32
    )
    keys_part = score_scale * jnp.einsum(
        "ghqk,qgha->kga", grad_scores, query_group, preferred_element_type=f32
    )
    values_part = jnp.einsum(
        "ghqk,qgha->kga", probs_low, grad_group, preferred_element_type=f32
    )
    key_value_part = jnp.concatenate(
        [keys_part.reshape(seq_length, key_width), values_part.reshape(seq_length, key_width)],
        axis=1,
    ).astype(bf16)
    key_value_grad = links.reduce_ring(blocks_of(key_value_part))
    grad_values = key_value_grad[:, key_width:]
    query_pre = unrotate(
        grad_query.reshape(tok_rows, HEADS, HEAD_DIM), cos_tab, sin_tab
    ).reshape(tok_rows, query_width)
    key_pre = unrotate(
        key_value_grad[:, :key_width].reshape(tok_rows, KV_HEADS, HEAD_DIM), cos_tab, sin_tab
    ).reshape(tok_rows, key_width)
    query_grad_low = query_pre.astype(bf16)
    key_value_grad_low = jnp.concatenate([key_pre, grad_values], axis=1).astype(bf16)
    grad_normed_one = dot_rows(query_grad_low, query_w) + dot_rows(key_value_grad_low, key_value_w)
    grad_inputs, attn_gain_part = norm_back(grad_normed_one, inputs, inv_one, attn_gain_all)
    in_grad = turn_cols(resid_grad + grad_inputs)

    mlp_out = links.reduce_ring(blocks_of(mlp_part))
    layer_out = turn_cols(resid_one + mlp_out)

    def ff_weight_grad(left_side, right_side):
        whole = dot_cols(left_side, right_side).astype(bf16)
        split_rows = whole.reshape(fsdp_count, groups_each, fsdp_count, rows_each, width)

        def owned_by(j):
            return lax.dynamic_index_in_dim(split_rows, fsdp_rank ^ j, 2, keepdims=False)

        def reblock(values, j):
            return jnp.concatenate([values[i ^ j : (i ^ j) + 1] for i in range(fsdp_count)], axis=0)

        send_far = owned_by(3)
        send_near = owned_by(1)
        got_far = reblock(links.core(send_far), 1)
        got_near = reblock(links.core(send_near), 1)
        across = reblock(links.chip(owned_by(2) + got_far), 2)
        total = (
            owned_by(0).astype(f32) + got_near.astype(f32) + across.astype(f32)
        ).astype(bf16)
        return total.reshape(ctx_count, rows_each, width)

    def to_owners(reduced):
        pieces = []
        for k in range(ctx_count):
            owner = ctx_rank ^ k
            at = ((owner // groups_each) ^ fsdp_rank) * groups_each + owner % groups_each
            piece = lax.dynamic_index_in_dim(reduced, at, 0, keepdims=False)
            if k:
                piece = lax.ppermute(piece, "ctx", [(i, i ^ k) for i in range(ctx_count)])
            pieces.append(piece)
        stack = jnp.stack(pieces)
        out = []
        for o in range(ctx_count):
            begin = min(span * o, tiles - span)
            skip = span * o - begin
            if skip >= span:
                continue
            part = lax.dynamic_index_in_dim(stack, ctx_rank ^ o, 0, keepdims=False)
            out.append(part[:, skip * LANES :])
        return jnp.concatenate(out, axis=1).astype(f32)

    down_weight_grad = to_owners(ff_weight_grad(grad_low_all, hidden))
    gate_weight_grad = to_owners(ff_weight_grad(normed_two_all, grad_gate))
    up_weight_grad = to_owners(ff_weight_grad(normed_two_all, grad_up))

    def owner_cols(values):
        natural = turn_cols(values).reshape(tok_rows, ctx_count, fsdp_count, rows_each)
        return jnp.transpose(natural, (2, 0, 1, 3)).reshape(
            fsdp_count, tok_rows, ctx_count * rows_each
        )

    def exchange_fsdp(by_owner):
        def owned_by(j):
            return lax.dynamic_index_in_dim(by_owner, fsdp_rank ^ j, 0, keepdims=False)

        near = links.core(owned_by(1))
        far = links.chip(jnp.concatenate([owned_by(2), owned_by(3)], axis=0))
        other = links.core(far[tok_rows:])
        return jnp.concatenate([owned_by(0), near, far[:tok_rows], other], axis=0)

    normed_owned = exchange_fsdp(owner_cols(normed_one))
    resid_owned = exchange_fsdp(owner_cols(resid_low))
    attn_out_all = jnp.concatenate(links.gather_fsdp(attn_out), axis=0)
    query_grad_all = jnp.concatenate(links.gather_fsdp(query_grad_low), axis=0)
    key_value_grad_all = jnp.concatenate(links.gather_fsdp(key_value_grad_low), axis=0)

    def ring_owned(partial):
        by_ctx = partial.astype(bf16).reshape(ctx_count, rows_each, partial.shape[1])
        return links.reduce_ring(
            [lax.dynamic_index_in_dim(by_ctx, at, 0, keepdims=False) for at in links.order]
        )

    out_weight_grad = ring_owned(dot_cols(resid_owned, attn_out_all))
    query_weight_grad = ring_owned(dot_cols(normed_owned, query_grad_all))
    key_value_weight_grad = ring_owned(dot_cols(normed_owned, key_value_grad_all))

    sums = jnp.concatenate(
        [
            turn_cols(attn_gain_part[None])[0],
            turn_cols(mlp_gain_part[None])[0],
            jnp.sum(query_pre, axis=0),
            jnp.sum(key_pre, axis=0),
            jnp.sum(grad_values, axis=0),
        ]
    )
    sums = sums + links.core(sums)
    sums = sums + links.chip(sums)
    step = 1
    while step < ctx_count:
        sums = sums + lax.ppermute(sums, "ctx", [(i, i ^ step) for i in range(ctx_count)])
        step *= 2
    owner_index = ctx_rank * fsdp_count + fsdp_rank

    def own_sum(begin, size):
        each = size // (ctx_count * fsdp_count)
        return lax.dynamic_slice_in_dim(sums[begin : begin + size], owner_index * each, each)

    at_bias = 2 * model_width
    return (
        layer_out[None],
        in_grad[None],
        own_sum(0, model_width),
        query_weight_grad,
        own_sum(at_bias, query_width),
        key_value_weight_grad[:, :key_width],
        own_sum(at_bias + query_width, key_width),
        key_value_weight_grad[:, key_width:],
        own_sum(at_bias + query_width + key_width, key_width),
        out_weight_grad,
        own_sum(model_width, model_width),
        gate_weight_grad,
        up_weight_grad,
        down_weight_grad,
    )


def solution(mesh):
    rows = P("fsdp", None)
    owned = P(("ctx", "fsdp"))
    owned_rows = P(("ctx", "fsdp"), None)
    tokens = P("fsdp", "ctx", None)
    in_specs = (
        tokens,
        P(),
        P("fsdp"),
        rows,
        P("fsdp"),
        rows,
        P("fsdp"),
        rows,
        P("fsdp"),
        rows,
        P("fsdp"),
        rows,
        rows,
        rows,
        tokens,
    )
    out_specs = (
        tokens,
        tokens,
        owned,
        owned_rows,
        owned,
        owned_rows,
        owned,
        owned_rows,
        owned,
        owned_rows,
        owned,
        owned_rows,
        owned_rows,
        owned_rows,
    )
    return jax.shard_map(shards, mesh=mesh, in_specs=in_specs, out_specs=out_specs, check_vma=False)
```

```python
import functools

import jax
import jax.numpy as jnp
import numpy as np
from jax import lax
from jax.experimental import pallas as pl
from jax.experimental.pallas import tpu as pltpu
from jax.sharding import PartitionSpec as P

HEADS = 12
KV_HEADS = 2
HEAD_DIM = 128
GROUP = HEADS // KV_HEADS

NORM_EPSILON = 1e-06
ROPE_THETA = 1000000.0
MASK_VALUE = -1e30
LANES = 128

bf16 = jnp.bfloat16
f32 = jnp.float32


def dot_plain(left_side, right_side):
    return jnp.dot(left_side, right_side, preferred_element_type=f32)


def dot_rows(left_side, right_side):
    return lax.dot_general(
        left_side, right_side, (((1,), (1,)), ((), ())), preferred_element_type=f32
    )


def dot_cols(left_side, right_side):
    return lax.dot_general(
        left_side, right_side, (((0,), (0,)), ((), ())), preferred_element_type=f32
    )


def pick(values, index, axis=0):
    return lax.dynamic_index_in_dim(
        values, index, axis, keepdims=False, allow_negative_indices=False
    )


def cut(values, start, size, axis=0):
    return lax.dynamic_slice_in_dim(values, start, size, axis, allow_negative_indices=False)


def after(values, *markers):
    return lax.optimization_barrier((values, markers))[0]


def rms_scale(values):
    return lax.rsqrt(jnp.mean(values * values, axis=-1, keepdims=True) + NORM_EPSILON)


def rope_tables(token_pos, head_dim):
    half_dim = head_dim // 2
    inv_freq = ROPE_THETA ** (jnp.arange(half_dim, dtype=f32) * (-2.0 / head_dim))
    angles = token_pos.astype(f32)[:, None] * inv_freq[None, :]
    angles = jnp.concatenate([angles, angles], axis=1)
    return (jnp.cos(angles), jnp.sin(angles))


def turned(heads_in):
    return pltpu.roll(heads_in, HEAD_DIM // 2, 1)


def small_row(small_refs, row, size):
    return [small[row : row + 1, :size].astype(f32) for small in small_refs]


def natural_bias(place_ref, small_refs, begin, size):
    pieces = [small[3:4, begin : begin + size].astype(f32) for small in small_refs]
    parts = []
    for block in range(4):
        part = pieces[0]
        for j in range(1, 4):
            part = jnp.where(piece_at(place_ref, j) == block, pieces[j], part)
        parts.append(part)
    return jnp.concatenate(parts, axis=1)


def piece_at(place_ref, j):
    return place_ref[place_ref.shape[0] - 4 + j]


def piece_cols(place_ref, j, depth):
    return pl.ds(pl.multiple_of(piece_at(place_ref, j) * depth, depth), depth)


def front_kernel(place_ref, x_ref, cos_ref, sin_ref, *refs):
    key_w, value_w, small, (normed_ref, key_value_ref) = refs[:4], refs[4:8], refs[8:12], refs[12:]
    depth = key_w[0].shape[0]
    gains = small_row(small, 0, depth)
    values = x_ref[...]
    inv_rms = rms_scale(values)
    keys, vals = 0.0, 0.0
    for j in range(4):
        cols = piece_cols(place_ref, j, depth)
        part = (x_ref[:, cols] * inv_rms * gains[j]).astype(bf16)
        normed_ref[:, cols] = part
        keys += dot_plain(part, key_w[j][...])
        vals += dot_plain(part, value_w[j][...])
    each = key_w[0].shape[1] // 4
    width = 4 * each
    keys = keys + natural_bias(place_ref, small, 0, each)
    vals = vals + natural_bias(place_ref, small, each, each)
    for g in range(KV_HEADS):
        cols = slice(g * HEAD_DIM, (g + 1) * HEAD_DIM)
        head = keys[:, cols]
        key_value_ref[:, cols] = (head * cos_ref[...] + turned(head) * sin_ref[...]).astype(bf16)
    key_value_ref[:, width:] = vals.astype(bf16)


def query_kernel(place_ref, normed_ref, cos_ref, sin_ref, *refs):
    query_w, small, (query_ref, lin) = refs[:4], refs[4:8], refs[8:]
    depth = query_w[0].shape[0]
    total = 0.0
    for j in range(4):
        total += dot_plain(normed_ref[:, piece_cols(place_ref, j, depth)], query_w[j][...])
    lin[...] = total
    bias = small_row(small, 2, depth)
    for j in range(4):
        lin[:, piece_cols(place_ref, j, depth)] += bias[j]
    for h in range(HEADS):
        cols = slice(h * HEAD_DIM, (h + 1) * HEAD_DIM)
        head = lin[:, cols]
        query_ref[:, cols] = (head * cos_ref[...] + turned(head) * sin_ref[...]).astype(bf16)


def block_positions(block_map_ref, index, rows, axis):
    half = rows // 2
    shape = (1, rows) if axis else (rows, 1)
    offset = lax.broadcasted_iota(jnp.int32, shape, axis)
    low = block_map_ref[2 * index] * half + offset
    high = block_map_ref[2 * index + 1] * half + (offset - half)
    return jnp.where(offset < half, low, high)


def head_cols(h):
    return slice(h * HEAD_DIM, (h + 1) * HEAD_DIM)


def join_keys(place_ref, block_map_ref, blocks, keys_v, pos_v):
    rows = blocks[0].shape[0]
    for i, block in enumerate(blocks):
        keys_v[i * rows : (i + 1) * rows] = block[...]
        pos_v[:, i * rows : (i + 1) * rows] = block_positions(
            block_map_ref, place_ref[i], rows, 1
        )


def attend_kernel(count, place_ref, block_map_ref, x_ref, query_ref, out_hbm, *refs):
    blocks, small = refs[:count], refs[count : count + 4]
    attn_ref, norm_ref, resid_ref, normed_ref, keys_v, pos_v, out_v, sem = refs[count + 4 :]
    load = pltpu.make_async_copy(out_hbm, out_v, sem)
    load.start()
    rows = query_ref.shape[0]
    width = KV_HEADS * HEAD_DIM
    join_keys(place_ref, block_map_ref, blocks, keys_v, pos_v)
    allowed = pos_v[...] <= block_positions(block_map_ref, place_ref[0], rows, 0)
    for h in range(HEADS):
        group = h // GROUP
        scores = dot_rows(query_ref[:, head_cols(h)], keys_v[:, head_cols(group)])
        scores = jnp.where(allowed, scores * HEAD_DIM ** (-0.5), MASK_VALUE)
        row_max = jnp.max(scores, axis=1, keepdims=True)
        raised = jnp.exp(scores - row_max)
        row_sum = jnp.sum(raised, axis=1, keepdims=True)
        norm_ref[h] = row_max + jnp.log(row_sum)
        probs_low = (raised * (1.0 / row_sum)).astype(bf16)
        values = keys_v[:, width + group * HEAD_DIM : width + (group + 1) * HEAD_DIM]
        attn_ref[:, head_cols(h)] = dot_plain(probs_low, values).astype(bf16)
    load.wait()
    resid_ref[...] = x_ref[...] + dot_rows(attn_ref[...], out_v[...])
    inv_rms = rms_scale(resid_ref[...])
    depth = x_ref.shape[1] // 4
    for j, gain in enumerate(small_row(small, 1, depth)):
        cols = piece_cols(place_ref, j, depth)
        normed_ref[:, cols] = (resid_ref[:, cols] * inv_rms * gain).astype(bf16)


def norm_back_refs(place_ref, gains, upstream_ref, values_ref, base_ref, out_ref, part_ref):
    depth = values_ref.shape[1] // 4
    inv_rms = rms_scale(values_ref[...])
    inner = 0.0
    for j in range(4):
        cols = piece_cols(place_ref, j, depth)
        inner += jnp.sum(
            upstream_ref[:, cols] * gains[j] * values_ref[:, cols], axis=1, keepdims=True
        )
    inner = inner * (inv_rms * inv_rms * inv_rms) * (1.0 / values_ref.shape[1])
    for j in range(4):
        cols = piece_cols(place_ref, j, depth)
        upstream, values = upstream_ref[:, cols], values_ref[:, cols]
        part_ref[:, cols] = jnp.sum(upstream * values * inv_rms, axis=0, keepdims=True)
        out_ref[:, cols] = base_ref[:, cols] + (inv_rms * (upstream * gains[j]) - values * inner)


def back_kernel(count, place_ref, block_map_ref, *refs):
    (
        own_ref,
        going_ref,
        coming_ref,
        resid_ref,
        cotangent_ref,
        attn_ref,
        query_ref,
        norm_ref,
        cos_ref,
        sin_ref,
        out_hbm,
    ) = refs[:11]
    blocks, small = refs[11 : 11 + count], refs[11 + count : 15 + count]
    refs = refs[15 + count :]
    grad_ref, low_ref, gain_ref, query_grad_ref, query_sum_ref = refs[:5]
    parts = refs[5 : 5 + count]
    keys_v, pos_v, out_v, upstream_v, attn_grad_v, scores_v, probs_v, sem = refs[5 + count :]
    load = pltpu.make_async_copy(out_hbm, out_v, sem)
    load.start()
    rows = query_ref.shape[0]
    width = KV_HEADS * HEAD_DIM
    scale = HEAD_DIM ** (-0.5)
    upstream_v[...] = (
        own_ref[...].astype(f32) + going_ref[...].astype(f32) + coming_ref[...].astype(f32)
    )
    gains = small_row(small, 1, resid_ref.shape[1] // 4)
    norm_back_refs(place_ref, gains, upstream_v, resid_ref, cotangent_ref, grad_ref, gain_ref)
    low_ref[...] = grad_ref[...].astype(bf16)
    join_keys(place_ref, block_map_ref, blocks, keys_v, pos_v)
    allowed = pos_v[...] <= block_positions(block_map_ref, place_ref[0], rows, 0)
    load.wait()
    attn_grad_v[...] = dot_plain(low_ref[...], out_v[...]).astype(bf16)
    for group in range(KV_HEADS):
        keys = keys_v[:, head_cols(group)]
        values = keys_v[:, width + group * HEAD_DIM : width + (group + 1) * HEAD_DIM]
        query_stack, grad_stack = [], []
        for n in range(GROUP):
            h = group * GROUP + n
            query, grad_out = query_ref[:, head_cols(h)], attn_grad_v[:, head_cols(h)]
            query_stack.append(query)
            grad_stack.append(grad_out)
            scores = jnp.where(allowed, dot_rows(query, keys) * scale, MASK_VALUE)
            prob = jnp.exp(scores - norm_ref[h])
            delta = jnp.sum(
                grad_out.astype(f32) * attn_ref[:, head_cols(h)].astype(f32),
                axis=1,
                keepdims=True,
            )
            grad_scores = (prob * (dot_rows(grad_out, values) - delta)).astype(bf16)
            stack_rows = slice(n * rows, (n + 1) * rows)
            scores_v[stack_rows] = grad_scores
            probs_v[stack_rows] = prob.astype(bf16)
            back = scale * dot_plain(grad_scores, keys)
            back = back * cos_ref[...] - turned(back) * sin_ref[...]
            query_sum_ref[:, head_cols(h)] = jnp.sum(back, axis=0, keepdims=True)
            query_grad_ref[:, head_cols(h)] = back.astype(bf16)
        key_part = (scale * dot_cols(scores_v[...], jnp.concatenate(query_stack, axis=0))).astype(
            bf16
        )
        value_part = dot_cols(probs_v[...], jnp.concatenate(grad_stack, axis=0)).astype(bf16)
        for i, part in enumerate(parts):
            part[:, head_cols(group)] = key_part[i * rows : (i + 1) * rows]
            part[:, width + group * HEAD_DIM : width + (group + 1) * HEAD_DIM] = value_part[
                i * rows : (i + 1) * rows
            ]


def last_kernel(place_ref, *refs):
    (
        own_ref,
        going_ref,
        coming_ref,
        x_ref,
        base_ref,
        query_grad_ref,
        cos_ref,
        sin_ref,
    ) = refs[:8]
    query_w, key_w, value_w, small = refs[8:12], refs[12:16], refs[16:20], refs[20:24]
    in_grad_ref, gain_ref, low_ref, sum_ref, upstream_v = refs[24:]
    depth = x_ref.shape[1] // 4
    width = KV_HEADS * HEAD_DIM
    total = own_ref[...].astype(f32) + going_ref[...].astype(f32) + coming_ref[...].astype(f32)
    for g in range(KV_HEADS):
        head = total[:, head_cols(g)]
        back = head * cos_ref[...] - turned(head) * sin_ref[...]
        sum_ref[:, head_cols(g)] = jnp.sum(back, axis=0, keepdims=True)
        low_ref[:, head_cols(g)] = back.astype(bf16)
    sum_ref[:, width:] = jnp.sum(total[:, width:], axis=0, keepdims=True)
    low_ref[:, width:] = total[:, width:].astype(bf16)
    for j in range(4):
        upstream_v[:, piece_cols(place_ref, j, depth)] = (
            dot_rows(query_grad_ref[...], query_w[j][...])
            + dot_rows(low_ref[:, :width], key_w[j][...])
            + dot_rows(low_ref[:, width:], value_w[j][...])
        )
    gains = small_row(small, 0, depth)
    norm_back_refs(place_ref, gains, upstream_v, x_ref, base_ref, in_grad_ref, gain_ref)


def local_call(kernel, name, scalars, arrays, outs, scratch=(), hbm=(), flops=0):
    moved = sum(a.size * a.dtype.itemsize for a in arrays)
    return pl.pallas_call(
        kernel,
        in_specs=[pl.BlockSpec(memory_space=pltpu.SMEM)] * len(scalars)
        + [
            pl.BlockSpec(memory_space=pl.ANY if i in hbm else pltpu.VMEM)
            for i in range(len(arrays))
        ],
        out_specs=[pl.BlockSpec(memory_space=pltpu.VMEM)] * len(outs),
        out_shape=[jax.ShapeDtypeStruct(shape, kind) for shape, kind in outs],
        scratch_shapes=list(scratch),
        compiler_params=pltpu.CompilerParams(vmem_limit_bytes=58 << 20),
        cost_estimate=pl.CostEstimate(flops=flops, bytes_accessed=moved, transcendentals=0),
        name=name,
    )(*scalars, *arrays)


def ff_kernel(blocks, aliased, place_ref, *refs):
    count = len(blocks)
    x_refs = refs[:count]
    grad_hidden_hbm = refs[count]
    gate_pieces, up_pieces = refs[count + 1 : count + 5], refs[count + 5 : count + 9]
    refs = refs[count + 9 + aliased :]
    outs, grad_outs = refs[:4], refs[4 : 4 + count]
    x_v, hidden_v, gate_grad_v, up_grad_v, grad_hidden_v, gate_v, up_v, out_sems, in_sems = refs[
        4 + count :
    ]
    rows, (depth, width) = x_refs[0].shape[0], gate_pieces[0].shape

    def go(source, target, sem):
        copy = pltpu.make_async_copy(source, target, sem)
        copy.start()
        return copy

    def stored(i):
        return pl.ds(pl.multiple_of(place_ref[blocks[i]] * rows, rows), rows)

    def here(i):
        return pl.ds(i * rows, rows)

    first_kept = place_ref[place_ref.shape[0] - 5]

    def piece_rows(j):
        start = place_ref[place_ref.shape[0] - 4 + j] * depth
        return pl.ds(pl.multiple_of(start, depth), depth)

    gate_in = [go(gate_pieces[j], gate_v.at[piece_rows(j)], in_sems.at[j]) for j in range(4)]
    up_in = [go(up_pieces[j], up_v.at[piece_rows(j)], in_sems.at[4 + j]) for j in range(4)]
    hidden_in = [
        go(grad_hidden_hbm.at[stored(i)], grad_hidden_v.at[here(i)], in_sems.at[8 + i])
        for i in range(count)
    ]
    for i in range(count):
        x_v[i * rows : (i + 1) * rows] = x_refs[i][...]
    going = [go(x_v.at[here(i)], outs[0].at[stored(i)], out_sems.at[0, i]) for i in range(count)]
    for copy in gate_in:
        copy.wait()
    gate_lin = dot_plain(x_v[...], gate_v[...])
    for copy in up_in:
        copy.wait()
    up_lin = dot_plain(x_v[...], up_v[...])
    for copy in hidden_in:
        copy.wait()
    grad_hidden = grad_hidden_v[...]
    kept = lax.broadcasted_iota(jnp.int32, (1, width), 1) >= first_kept
    sig_gate = 1.0 / (1.0 + jnp.exp(-gate_lin))
    activated = gate_lin * sig_gate
    gate_grad_v[...] = jnp.where(
        kept, grad_hidden * up_lin * (sig_gate * (1.0 + gate_lin * (1.0 - sig_gate))), 0.0
    ).astype(bf16)
    up_grad_v[...] = jnp.where(kept, grad_hidden * activated, 0.0).astype(bf16)
    hidden_v[...] = jnp.where(kept, activated * up_lin, 0.0).astype(bf16)
    for n, held in enumerate((hidden_v, gate_grad_v, up_grad_v)):
        going += [
            go(held.at[here(i)], outs[n + 1].at[stored(i)], out_sems.at[n + 1, i])
            for i in range(count)
        ]
    low = (dot_rows(gate_grad_v[...], gate_v[...]) + dot_rows(up_grad_v[...], up_v[...])).astype(
        bf16
    )
    for i in range(count):
        grad_outs[i][...] = low[i * rows : (i + 1) * rows]
    for copy in going:
        copy.wait()


def ff_rows(blocks, length, place, x_blocks, grad_hidden, gate_pieces, up_pieces, held):
    rows, model_width = x_blocks[0].shape
    width = gate_pieces[0].shape[1]
    count = len(blocks)
    total = count * rows
    in_vmem = pl.BlockSpec(memory_space=pltpu.VMEM)
    in_place = pl.BlockSpec(memory_space=pl.ANY)
    aliased = 4 if held else 0
    outs = pl.pallas_call(
        functools.partial(ff_kernel, blocks, aliased),
        in_specs=[pl.BlockSpec(memory_space=pltpu.SMEM)]
        + [in_vmem] * count
        + [in_place] * (9 + aliased),
        out_specs=[in_place] * 4 + [in_vmem] * count,
        scratch_shapes=[pltpu.VMEM((total, model_width), bf16)]
        + [pltpu.VMEM((total, width), bf16)] * 3
        + [pltpu.VMEM((total, width), f32)]
        + [pltpu.VMEM((model_width, width), bf16)] * 2
        + [pltpu.SemaphoreType.DMA((4, count)), pltpu.SemaphoreType.DMA((8 + count,))],
        out_shape=[jax.ShapeDtypeStruct((length, model_width), bf16)]
        + [jax.ShapeDtypeStruct((length, width), bf16)] * 3
        + [jax.ShapeDtypeStruct((rows, model_width), bf16)] * count,
        input_output_aliases={count + 10 + i: i for i in range(aliased)},
        compiler_params=pltpu.CompilerParams(vmem_limit_bytes=40 << 20),
        cost_estimate=pl.CostEstimate(
            flops=8 * total * model_width * width,
            bytes_accessed=4 * model_width * width + 8 * total * model_width,
            transcendentals=total * width,
        ),
        name="ff_rows_%d" % blocks[0],
    )(place, *x_blocks, grad_hidden, *gate_pieces, *up_pieces, *held)
    return tuple(outs[:4]), list(outs[4:])


def place_kernel(place_ref, *refs):
    blocks, whole, sems = refs[:-2], refs[-2], refs[-1]
    rows = blocks[0].shape[0]
    copies = []
    for i, block in enumerate(blocks):
        start = pl.multiple_of(place_ref[i] * rows, rows)
        copies.append(pltpu.make_async_copy(block, whole.at[pl.ds(start, rows)], sems.at[i]))
        copies[-1].start()
    for copy in copies:
        copy.wait()


def place_blocks(blocks, place):
    rows, columns = blocks[0].shape
    count = len(blocks)
    return pl.pallas_call(
        place_kernel,
        in_specs=[pl.BlockSpec(memory_space=pltpu.SMEM)]
        + [pl.BlockSpec(memory_space=pltpu.VMEM)] * count,
        out_specs=pl.BlockSpec(memory_space=pl.ANY),
        scratch_shapes=[pltpu.SemaphoreType.DMA((count,))],
        out_shape=jax.ShapeDtypeStruct((count * rows, columns), blocks[0].dtype),
        cost_estimate=pl.CostEstimate(
            flops=0, bytes_accessed=8 * count * rows * columns, transcendentals=0
        ),
        name="place_blocks",
    )(place, *blocks)


class Links:
    def __init__(self, extra):
        self.count = lax.axis_size("ctx")
        self.rank = lax.axis_index("ctx")
        self.seq = lax.axis_index("fsdp")
        count = self.count
        if count == 8:
            self.ring = [0, 2, 4, 6, 7, 5, 3, 1]
        else:
            self.ring = list(range(count))
        following = {self.ring[i]: self.ring[(i + 1) % count] for i in range(count)}
        self.ahead = [(i, following[i]) for i in range(count)]
        self.back = [(following[i], i) for i in range(count)]
        place = [self.ring.index(i) for i in range(count)]
        half = count // 2
        self.offsets = [0] + [s * k for k in range(1, half) for s in (1, -1)] + [half]
        ranks = [
            [self.ring[(place[rank] + off) % count] for off in self.offsets]
            for rank in range(count)
        ]
        table = np.array(
            [
                ranks[rank] + extra(rank) + [seq ^ j for j in range(4)]
                for rank in range(count)
                for seq in range(4)
            ],
            np.int32,
        )
        self.place = lax.dynamic_slice(
            jnp.asarray(table),
            (self.rank * 4 + self.seq, 0),
            (1, table.shape[1]),
            allow_negative_indices=False,
        ).reshape(-1)
        self.order = [self.place[i] for i in range(count)]

    def forward(self, values):
        return lax.ppermute(values, "ctx", self.ahead)

    def backward(self, values):
        return lax.ppermute(values, "ctx", self.back)

    def core(self, values):
        return lax.ppermute(values, "fsdp", [(i, i ^ 1) for i in range(4)])

    def chip(self, values):
        return lax.ppermute(values, "fsdp", [(i, i ^ 2) for i in range(4)])

    def gather_fsdp(self, values):
        near = self.core(values)
        far = self.chip(values)
        return [values, near, far, self.core(far)]

    def bit(self, values, step):
        return lax.ppermute(values, "ctx", [(i, i ^ step) for i in range(self.count)])

    def bits(self):
        return [1 << k for k in range(self.count.bit_length() - 1)]

    def reduce_bits(self, chunk):
        held = {q: chunk(q).astype(f32) for q in range(self.count)}
        for step in self.bits():
            keys = sorted(q for q in held if q & step)
            got = self.bit(jnp.stack([held.pop(q) for q in keys]).astype(bf16), step)
            for i, q in enumerate(keys):
                held[q ^ step] = held[q ^ step] + got[i].astype(f32)
        return held[0]

    def gather_ring(self, values):
        half_rows = values.shape[0] // 2
        half = self.count // 2
        found = {0: values}
        going, coming = values, values
        for k in range(1, half):
            going, coming = self.forward(going), self.backward(coming)
            found[-k], found[k] = going, coming
        far_low = self.forward(going[:half_rows])
        far_high = self.backward(coming[half_rows:])
        found[half] = jnp.concatenate([far_low, far_high], axis=0)
        return [found[off] for off in self.offsets]

    def reduce_ring(self, blocks):
        part = dict(zip(self.offsets, blocks))
        half = self.count // 2
        half_rows = blocks[0].shape[0] // 2
        going = self.forward(part[half][:half_rows])
        coming = self.backward(part[half][half_rows:])
        top, bottom = part[half - 1], part[1 - half]
        going = jnp.concatenate([top[:half_rows] + going, top[half_rows:]], axis=0)
        coming = jnp.concatenate([bottom[:half_rows], bottom[half_rows:] + coming], axis=0)
        for k in range(half - 2, -1, -1):
            going, coming = self.forward(going), self.backward(coming)
            if k:
                going, coming = going + part[k], coming + part[-k]
        return part[0], going, coming


def shards(
    layer_in,
    block_map,
    attn_gain,
    query_weight,
    query_bias,
    key_weight,
    key_bias,
    value_weight,
    value_bias,
    out_weight,
    mlp_gain,
    gate_weight,
    up_weight,
    down_weight,
    out_grad,
):
    tiles = gate_weight.shape[1] // LANES
    span = -(-tiles // lax.axis_size("ctx"))

    def window(rank):
        begin = min(span * rank, tiles - span)
        return [begin * LANES, (span * rank - begin) * LANES]

    links = Links(window)
    ctx_count, fsdp_count = links.count, 4
    ctx_rank, fsdp_rank = links.rank, links.seq
    tok_rows, model_width = layer_in.shape[1:]
    block_len = tok_rows // 2
    seq_length = tok_rows * ctx_count
    query_width = HEADS * HEAD_DIM
    key_width = KV_HEADS * HEAD_DIM
    quarter = model_width // fsdp_count
    rows_each = model_width // (ctx_count * fsdp_count)
    groups_each = ctx_count // fsdp_count

    width = span * LANES

    def ff_slice(weight):
        return cut(weight, links.place[ctx_count], width, 1)

    inputs = layer_in[0]
    cotangent = out_grad[0]
    grad_low = cotangent.astype(bf16)

    key_all = links.gather_fsdp(key_weight)
    value_all = links.gather_fsdp(value_weight)
    small_msg = jnp.stack(
        [
            jnp.pad(row, (0, quarter - row.shape[0]))
            for row in (
                attn_gain,
                mlp_gain,
                query_bias,
                jnp.concatenate([key_bias, value_bias]),
            )
        ]
    )
    small_all = links.gather_fsdp(small_msg)
    query_all = links.gather_fsdp(query_weight)

    def whole_rows(weight):
        return lax.all_gather(weight, "fsdp", axis=0, tiled=True)

    gate_pieces = links.gather_fsdp(ff_slice(gate_weight))
    up_pieces = links.gather_fsdp(ff_slice(up_weight))

    token_pos = (
        jnp.repeat(cut(block_map, 2 * ctx_rank, 2), block_len, total_repeat_length=tok_rows)
        * block_len
        + jnp.arange(tok_rows, dtype=jnp.int32) % block_len
    )
    cos_tab, sin_tab = rope_tables(token_pos, HEAD_DIM)
    sin_tab = jnp.where(jnp.arange(HEAD_DIM)[None, :] < HEAD_DIM // 2, -sin_tab, sin_tab)

    wide_low = ((tok_rows, model_width), bf16)
    wide_full = ((tok_rows, model_width), f32)
    key_value_kind = ((tok_rows, 2 * key_width), bf16)
    normed_one, key_value = local_call(
        front_kernel,
        "front",
        (links.place,),
        (inputs, cos_tab, sin_tab, *key_all, *value_all, *small_all),
        (wide_low, key_value_kind),
        flops=4 * tok_rows * model_width * key_width,
    )
    key_value_blocks = links.gather_ring(key_value)
    (query_low,) = local_call(
        query_kernel,
        "query",
        (links.place,),
        (normed_one, cos_tab, sin_tab, *query_all, *small_all),
        (((tok_rows, query_width), bf16),),
        (pltpu.VMEM((tok_rows, query_width), f32),),
        flops=2 * tok_rows * model_width * query_width,
    )
    out_w = whole_rows(after(out_weight, query_all[2]))
    down_w = whole_rows(after(ff_slice(down_weight), query_all[2]))
    attn_out, log_norm, resid_one, normed_two = local_call(
        functools.partial(attend_kernel, ctx_count),
        "attend",
        (links.place, block_map),
        (inputs, query_low, out_w, *key_value_blocks, *small_all),
        (
            ((tok_rows, query_width), bf16),
            ((HEADS, tok_rows, 1), f32),
            wide_full,
            wide_low,
        ),
        (
            pltpu.VMEM((seq_length, 2 * key_width), bf16),
            pltpu.VMEM((1, seq_length), jnp.int32),
            pltpu.VMEM((model_width, query_width), bf16),
            pltpu.SemaphoreType.DMA,
        ),
        hbm=(2,),
        flops=2 * tok_rows * query_width * (2 * seq_length + model_width),
    )
    grad_low_blocks = links.gather_ring(grad_low)

    def in_stored_order(blocks):
        return place_blocks(blocks, links.place)

    grad_low_all = in_stored_order(grad_low_blocks)
    grad_hidden = dot_plain(grad_low_all, down_w)
    arrived = dict(zip(links.offsets, links.gather_ring(normed_two)))
    half = ctx_count // 2
    held = ()
    grad_blocks = {}
    for group in [(0, 1, -1)] + [(k, -k) for k in range(2, half)] + [(half,)]:
        held, found = ff_rows(
            tuple(links.offsets.index(off) for off in group),
            seq_length,
            links.place,
            [arrived[off] for off in group],
            grad_hidden,
            gate_pieces,
            up_pieces,
            held,
        )
        grad_blocks.update(zip(group, found))
    normed_two_all, hidden, grad_gate, grad_up = held
    grad_normed_terms = links.reduce_ring([grad_blocks[off] for off in links.offsets])

    def to_fsdp_owners(left_side, right_side):
        whole = dot_cols(left_side, right_side).astype(bf16)
        split_rows = whole.reshape(ctx_count, fsdp_count, rows_each, width)

        def owned_by(j):
            return pick(split_rows, fsdp_rank ^ j, 1)

        from_core = links.core(jnp.stack([owned_by(3), owned_by(1)]))
        across = links.chip(owned_by(2) + from_core[0])
        return (owned_by(0), from_core[1], across)

    down_terms = to_fsdp_owners(grad_low_all, hidden)
    gate_terms = to_fsdp_owners(normed_two_all, grad_gate)
    up_terms = to_fsdp_owners(normed_two_all, grad_up)
    mlp_part = after(dot_rows(hidden, down_w).astype(bf16), *grad_normed_terms)
    mlp_out = lax.psum_scatter(mlp_part, "ctx", scatter_dimension=0, tiled=True)

    resid_grad, resid_low, mlp_gain_part, query_grad_low, query_sum, *key_value_parts = local_call(
        functools.partial(back_kernel, ctx_count),
        "back",
        (links.place, block_map),
        (
            *grad_normed_terms,
            resid_one,
            cotangent,
            attn_out,
            query_low,
            log_norm,
            cos_tab,
            sin_tab,
            out_w,
            *key_value_blocks,
            *small_all,
        ),
        (
            wide_full,
            wide_low,
            ((1, model_width), f32),
            ((tok_rows, query_width), bf16),
            ((1, query_width), f32),
        )
        + (key_value_kind,) * ctx_count,
        (
            pltpu.VMEM((seq_length, 2 * key_width), bf16),
            pltpu.VMEM((1, seq_length), jnp.int32),
            pltpu.VMEM((model_width, query_width), bf16),
            pltpu.VMEM((tok_rows, model_width), f32),
            pltpu.VMEM((tok_rows, query_width), bf16),
            pltpu.VMEM((GROUP * tok_rows, seq_length), bf16),
            pltpu.VMEM((GROUP * tok_rows, seq_length), bf16),
            pltpu.SemaphoreType.DMA,
        ),
        hbm=(10,),
        flops=2 * tok_rows * query_width * (5 * seq_length + model_width),
    )
    key_value_terms = links.reduce_ring(key_value_parts)
    in_grad, attn_gain_part, key_value_grad_low, key_value_sum = local_call(
        last_kernel,
        "last",
        (links.place,),
        (
            *key_value_terms,
            inputs,
            resid_grad,
            query_grad_low,
            cos_tab,
            sin_tab,
            *query_all,
            *key_all,
            *value_all,
            *small_all,
        ),
        (
            wide_full,
            ((1, model_width), f32),
            key_value_kind,
            ((1, 2 * key_width), f32),
        ),
        (pltpu.VMEM((tok_rows, model_width), f32),),
        flops=2 * tok_rows * model_width * (query_width + 2 * key_width),
    )

    def to_owners(terms, *markers):
        own, near, across = terms
        across = after(across, *markers)
        reduced = (own.astype(f32) + near.astype(f32) + across.astype(f32)).astype(bf16)
        stack = lax.all_to_all(reduced, "ctx", 0, 0)
        out = []
        for o in range(ctx_count):
            skip = window(o)[1]
            if skip < width:
                out.append(stack[o][:, skip:])
        return jnp.concatenate(out, axis=1).astype(f32)

    down_weight_grad = to_owners(down_terms, *grad_normed_terms)
    gate_weight_grad = to_owners(gate_terms, query_grad_low)
    up_weight_grad = to_owners(up_terms, query_grad_low)
    layer_out = resid_one + after(mlp_out, in_grad).astype(f32)

    def owner_cols(values):
        natural = values.reshape(tok_rows, ctx_count, fsdp_count, rows_each)
        return jnp.transpose(natural, (2, 0, 1, 3)).reshape(
            fsdp_count, tok_rows, ctx_count * rows_each
        )

    def exchange_fsdp(by_owner):
        def owned_by(j):
            return pick(by_owner, fsdp_rank ^ j)

        near = links.core(owned_by(1))
        far = links.chip(jnp.concatenate([owned_by(2), owned_by(3)], axis=0))
        other = links.core(far[tok_rows:])
        return jnp.concatenate([owned_by(0), near, far[:tok_rows], other], axis=0)

    normed_owned = exchange_fsdp(owner_cols(normed_one))
    resid_owned = exchange_fsdp(owner_cols(resid_low))
    attn_out_all = jnp.concatenate(links.gather_fsdp(attn_out), axis=0)
    query_grad_all = jnp.concatenate(links.gather_fsdp(query_grad_low), axis=0)
    key_value_grad_all = jnp.concatenate(links.gather_fsdp(key_value_grad_low), axis=0)

    def by_ctx(partial):
        return partial.astype(bf16).reshape(ctx_count, rows_each, partial.shape[1])

    wide = by_ctx(
        jnp.concatenate(
            [dot_cols(resid_owned, attn_out_all), dot_cols(normed_owned, query_grad_all)], axis=1
        )
    )
    wide_terms = links.reduce_ring([pick(wide, at) for at in links.order])
    wide_grad = sum(term.astype(f32) for term in wide_terms)
    out_weight_grad = wide_grad[:, :query_width]
    query_weight_grad = wide_grad[:, query_width:]
    narrow = by_ctx(dot_cols(normed_owned, key_value_grad_all))
    key_value_weight_grad = links.reduce_bits(
        lambda q: pick(narrow, ctx_rank ^ q)
    )

    sums = jnp.concatenate([attn_gain_part, mlp_gain_part, query_sum, key_value_sum], axis=1)
    sums = sums + links.core(sums)
    sums = sums + links.chip(sums)
    for step in links.bits():
        sums = sums + links.bit(sums, step)
    owner_index = ctx_rank * fsdp_count + fsdp_rank

    def own_sum(begin, size):
        each = size // (ctx_count * fsdp_count)
        return cut(sums[0, begin : begin + size], owner_index * each, each)

    at_bias = 2 * model_width
    return (
        layer_out[None],
        in_grad[None],
        own_sum(0, model_width),
        query_weight_grad,
        own_sum(at_bias, query_width),
        key_value_weight_grad[:, :key_width],
        own_sum(at_bias + query_width, key_width),
        key_value_weight_grad[:, key_width:],
        own_sum(at_bias + query_width + key_width, key_width),
        out_weight_grad,
        own_sum(model_width, model_width),
        gate_weight_grad,
        up_weight_grad,
        down_weight_grad,
    )


def solution(mesh):
    rows = P("fsdp", None)
    owned = P(("ctx", "fsdp"))
    owned_rows = P(("ctx", "fsdp"), None)
    tokens = P("fsdp", "ctx", None)
    in_specs = (
        tokens,
        P(),
        P("fsdp"),
        rows,
        P("fsdp"),
        rows,
        P("fsdp"),
        rows,
        P("fsdp"),
        rows,
        P("fsdp"),
        rows,
        rows,
        rows,
        tokens,
    )
    out_specs = (
        tokens,
        tokens,
        owned,
        owned_rows,
        owned,
        owned_rows,
        owned,
        owned_rows,
        owned,
        owned_rows,
        owned,
        owned_rows,
        owned_rows,
        owned_rows,
    )
    return jax.shard_map(shards, mesh=mesh, in_specs=in_specs, out_specs=out_specs, check_vma=False)
```
